512 devices in a mesh: mp: 2 (over y_hi), tok: 8 (over x, core), lat: 32 (over z, y_lo).
Axes of the slice: x: 4, y: 4 (y_hi: 2, y_lo: 2; y = y_hi * 2 + y_lo), z: 16, core: 2. Of those that a mesh axis runs over, the one named last changes fastest.
Arguments:
- inputs: bfloat16 [2, 384, 4608], P('mp', 'lat', 'tok'), may hold values from -6 to 6
- gate_w: bfloat16 [2, 4608, 18432], P('mp', 'tok', 'lat'), may hold values from -0.09375 to 0.09375
- up_w: bfloat16 [2, 4608, 18432], P('mp', 'tok', 'lat'), may hold values from -0.09375 to 0.09375
- down_w: bfloat16 [2, 18432, 4608], P('mp', 'lat', 'tok'), may hold values from -0.046875 to 0.046875
- enc_w: bfloat16 [2, 4608, 8192], P('mp', 'tok', 'lat'), may hold values from -0.0625 to 0.0625
- enc_bias: float32 [8192], P('lat'), may hold values from -3 to 3
- dec_w: bfloat16 [8192, 2, 4608], P('lat', 'mp', 'tok'), may hold values from -0.0625 to 0.0625
- dec_bias: float32 [2, 4608], P('mp', 'tok'), may hold values from -3 to 3
Outputs:
- recon_error: float32 [2, 384, 4608], P('mp', 'lat', 'tok')
- dec_grad: float32 [8192, 2, 4608], P('lat', 'mp', 'tok')
- latent_grad: float32 [384, 8192], P(None, 'lat')
The draws below stay inside these ranges and needn't reach their ends.
All inputs are finite; a program needn't handle non-finite values.
Results may differ from the reference program's by a relative error of at most 0.009.
Values may be sent and summed in bfloat16 or wider, within the bound.
A program may use at most 64 MiB of HBM per device.

```python
import jax
import jax.numpy as jnp

D = 4608
FF = 18432
LAT = 8192
TOKENS = 384


def levels(own_key, extent, pieces, smallest, high):
    def one(dim, parts):
        steps = jax.random.uniform(jax.random.fold_in(jax.random.fold_in(own_key, 6), dim), (parts,), jnp.float32, smallest / len(pieces), high / len(pieces))
        return jnp.repeat(jnp.exp(steps), extent[dim] // parts).reshape((-1,) + (1,) * (len(extent) - dim - 1))

    gain = one(*pieces[0])
    for cut in pieces[1:]:
        gain = gain * one(*cut)
    return gain


def normal_values(stream_key, extent, spread, reach, cuts=(), dtype=jnp.bfloat16):
    drawn = spread * jax.random.normal(stream_key, extent, jnp.float32)
    if cuts:
        drawn = drawn * levels(stream_key, extent, cuts, -0.22, 0.18)
    return jnp.clip(drawn, -reach, reach).astype(dtype)


def setup_inputs(seed: int = 0) -> dict:
    seeds = jax.random.split(jax.random.key(seed), 9)
    return {
        "inputs": normal_values(seeds[0], (2, TOKENS, D), 1.0, 6.0, ((0, 2), (1, 32), (2, 8))),
        "gate_w": normal_values(seeds[1], (2, D, FF), D ** -0.5, 0.09375, ((0, 2), (1, 8), (2, 32))),
        "up_w": normal_values(seeds[2], (2, D, FF), D ** -0.5, 0.09375, ((0, 2), (1, 8), (2, 32))),
        "down_w": normal_values(seeds[3], (2, FF, D), FF ** -0.5, 0.046875, ((0, 2), (1, 32), (2, 8))),
        "enc_w": normal_values(seeds[4], (2, D, LAT), (2 * D) ** -0.5, 0.0625, ((0, 2), (1, 8), (2, 32))),
        "enc_bias": normal_values(seeds[5], (LAT,), 0.5, 3.0, ((0, 32),), jnp.float32),
        "dec_w": normal_values(seeds[6], (LAT, 2, D), LAT ** -0.5, 0.0625, ((0, 32), (1, 2), (2, 8))),
        "dec_bias": normal_values(seeds[7], (2, D), 0.5, 3.0, ((0, 2), (1, 8)), jnp.float32),
    }


def reference(inputs, gate_w, up_w, down_w, enc_w, enc_bias, dec_w, dec_bias):
    acts = []
    for model in range(2):
        x_full = inputs[model]
        gate = jnp.dot(x_full, gate_w[model], preferred_element_type=jnp.float32)
        up_sum = jnp.dot(x_full, up_w[model], preferred_element_type=jnp.float32)
        hidden = (jax.nn.gelu(gate, approximate=True) * up_sum).astype(jnp.bfloat16)
        acts.append(jnp.dot(hidden, down_w[model], preferred_element_type=jnp.float32).astype(jnp.bfloat16))
    pre = jnp.dot(acts[0], enc_w[0], preferred_element_type=jnp.float32) + jnp.dot(acts[1], enc_w[1], preferred_element_type=jnp.float32) + enc_bias
    codes = jnp.maximum(pre, 0.0).astype(jnp.bfloat16)
    errors = []
    grads = []
    latent_grad = jnp.zeros((TOKENS, LAT), jnp.float32)
    for model in range(2):
        decoder = dec_w[:, model, :]
        recon = jnp.dot(codes, decoder, preferred_element_type=jnp.float32) + dec_bias[model]
        error = recon - acts[model].astype(jnp.float32)
        errors.append(error)
        error_b = error.astype(jnp.bfloat16)
        grads.append(jnp.dot(codes.T, error_b, preferred_element_type=jnp.float32))
        latent_grad = latent_grad + jnp.dot(error_b, decoder.T, preferred_element_type=jnp.float32)
    return jnp.stack(errors), jnp.stack(grads, axis=1), latent_grad
```

```python
import itertools

import jax
import jax.numpy as jnp
from jax import lax
from jax.experimental import pallas as pl
from jax.experimental.pallas import tpu as pltpu
from jax.sharding import PartitionSpec as P

MESH = pl.DeviceIdType.MESH
F32, BF16 = jnp.float32, jnp.bfloat16
GELU = 0.7978845608028654


def dot(a, b, ca=1, cb=0):
    return lax.dot_general(a, b, (((ca,), (cb,)), ((), ())), preferred_element_type=F32)


def gelu(v):
    return 0.5 * v * (1.0 + jnp.tanh(GELU * (v + 0.044715 * v * v * v)))


def kernel(
    x_hbm, gate_hbm, up_hbm, down_hbm, enc_hbm, ebias_hbm, dect_hbm, dbias_hbm,
    err_ref, gradt_ref, lat_ref,
    x_ref, gate_ref, up_ref, down_ref, enc_ref, ebias_ref, dect_ref, dbias_ref,
    xpair, xall,
    part, bcore, bsum, brecv, hid,
    dpart, dnear, dsum, dfar, acts,
    gpart, gnear, gsum, gfar, err,
    fpart, frecv, codes, ipart, irecv, lgrad,
    ssem, rsem, lsem,
):
    mp, tok, lat = lax.axis_index("mp"), lax.axis_index("tok"), lax.axis_index("lat")
    z, yl = lat // 2, lat % 2
    r, k = z % 4, z // 4
    xc, core = tok // 2, tok % 2
    q = mp * 8 + tok

    def at_z(d, y=None):
        return (mp, tok, ((z + d + 16) % 16) * 2 + (yl if y is None else y))

    def at_x(d):
        return (mp, ((xc + d) % 4) * 2 + core, lat)

    def at_q(d):
        o = (q + d) % 16
        return (o // 8, o % 8, lat)

    y_mate = (mp, tok, z * 2 + 1 - yl)
    core_mate = (mp, xc * 2 + 1 - core, lat)

    barrier = pltpu.get_barrier_semaphore()
    peers = [at_z(d) for d in (8, 4, 12)] + [at_z(d, y) for d in (2, -2, 1, -1) for y in range(2)]
    peers += [y_mate] + [at_q(d) for d in range(1, 16)]
    for peer in peers:
        pl.semaphore_signal(barrier, inc=1, device_id=peer, device_id_type=MESH)

    fetches = [
        pltpu.make_async_copy(src, dst, lsem.at[i])
        for i, (src, dst) in enumerate(
            (
                (x_hbm, x_ref), (gate_hbm, gate_ref), (up_hbm, up_ref), (down_hbm, down_ref),
                (enc_hbm, enc_ref), (ebias_hbm, ebias_ref), (dect_hbm, dect_ref), (dbias_hbm, dbias_ref),
            )
        )
    ]
    for fetch in fetches:
        fetch.start()

    count = [0]
    sent, awaited, landed, here = [], [], set(), set()

    def slots(n):
        count[0] += n
        return count[0] - n

    def send(src, dst, peer, out, into):
        copy = pltpu.make_async_remote_copy(
            src_ref=src, dst_ref=dst, send_sem=ssem.at[out], recv_sem=rsem.at[into], device_id=peer, device_id_type=MESH
        )
        copy.start()
        sent.append(copy)

    def coming(landing, slot):
        copy = pltpu.make_async_remote_copy(
            src_ref=landing, dst_ref=landing, send_sem=ssem.at[slot], recv_sem=rsem.at[slot], device_id=y_mate, device_id_type=MESH
        )
        awaited.append(copy)
        return copy

    def trade(src, dst, peer, landing):
        slot = slots(1)
        send(src, dst, peer, slot, slot)
        return coming(landing, slot)

    def land(copies):
        for copy in copies:
            landed.add(id(copy))
            copy.wait_recv()

    def fetched(*numbers):
        for i in numbers:
            if i not in here:
                here.add(i)
                fetches[i].wait()

    def finish():
        land([copy for copy in awaited if id(copy) not in landed])
        fetched(*range(len(fetches)))
        for copy in sent:
            copy.wait_send()

    def flat(v, width):
        return v.astype(F32).reshape(192, width).astype(BF16)

    def gather_inputs(buf):
        up1, down1, two = slots(4), slots(4), slots(4)
        far = {}
        for off in (2, 3, 1):
            c = (k + 4 - off) % 4
            own = buf.at[r, k // 2, k % 2]
            far[off] = trade(own, own, at_z(4 * off), buf.at[r, c // 2, c % 2])
        for off in (0, 3, 1, 2):
            c = (k + 4 - off) % 4
            if off:
                land([far[off]])
            piece = buf.at[r, c // 2, c % 2]
            send(piece, piece, at_z(2 - 4 * (c // 2)), two + c, two + c)
            send(piece, piece, at_z(1), up1 + c, up1 + c)
            send(piece, piece, at_z(-1), down1 + c, down1 + c)
        for c in range(4):
            land([
                coming(buf.at[(r + 3) % 4, c // 2, c % 2], up1 + c),
                coming(buf.at[(r + 1) % 4, c // 2, c % 2], down1 + c),
                coming(buf.at[(r + 2) % 4, c // 2, c % 2], two + c),
            ])

    def reduce_start(p, near, h):
        base = slots(7)
        for i, d in enumerate((-2 if h == 0 else 2, 1, -1)):
            for y in range(2):
                s = 2 * i + yl
                send(p.at[(r + d + 4) % 4, y], near.at[s], at_z(d, y), base + 2 * i + y, base + s)
        send(p.at[r, 1 - yl], near.at[6], y_mate, base + 6, base + 6)
        return [coming(near.at[s], base + s) for s in range(7)]

    def far_start(p, near, copies, total, far):
        land(copies)
        acc = p[r, yl].astype(F32)
        for s in range(7):
            acc = acc + near[s].astype(F32)
        total[...] = acc.astype(BF16)
        return [trade(total, far.at[off - 1], at_z(4 * off), far.at[off - 1]) for off in (2, 1, 3)]

    def far_sum(copies, total, far):
        land(copies)
        return total[...].astype(F32) + far[0].astype(F32) + far[1].astype(F32) + far[2].astype(F32)

    def spread_start(buf, h):
        base = slots(7)
        own = buf.at[r, yl]
        copies = []
        for i, d in enumerate((2 if h == 0 else -2, 1, -1)):
            for y in range(2):
                send(own, own, at_z(d, y), base + 2 * i + y, base + 2 * i + yl)
                copies.append(coming(buf.at[(r - d + 4) % 4, y], base + 2 * i + y))
        return copies + [trade(own, own, y_mate, buf.at[r, 1 - yl])]

    def scatter_start(p, recv):
        copies = []
        for d in range(1, 16):
            o = (q + d) % 16
            copies.append(trade(p.at[o // 8, o % 8], recv.at[d - 1], at_q(d), recv.at[d - 1]))
        return copies

    def scatter_sum(copies, p, recv):
        acc = p[mp, tok].astype(F32)
        for d, copy in enumerate(copies):
            land([copy])
            acc = acc + recv[d].astype(F32)
        return acc

    def gather_start(buf):
        own = buf.at[mp, tok]
        copies = []
        for d in range(1, 16):
            o = (q + 16 - d) % 16
            copies.append(trade(own, own, at_q(d), buf.at[o // 8, o % 8]))
        return copies

    def split(v):
        v = v.reshape(8, 24, 256)
        return v[:, :, :128].astype(BF16), v[:, :, 128:].astype(BF16)

    def join(buf):
        return jnp.concatenate([flat(buf[0], 128), flat(buf[1], 128)], axis=1)

    def chain(h):
        block = flat(xall[:, :, h], 576)
        fetched(1)
        part[h, 0] = dot(block, gate_ref[...]).reshape(4, 2, 24, 576).astype(BF16)
        cores = [trade(part.at[h, 0, :, 1 - core], bcore.at[h, 0], core_mate, bcore.at[h, 0])]
        fetched(2)
        part[h, 1] = dot(block, up_ref[...]).reshape(4, 2, 24, 576).astype(BF16)
        cores += [trade(part.at[h, 1, :, 1 - core], bcore.at[h, 1], core_mate, bcore.at[h, 1])]
        yield "b_dot"
        land(cores)
        for g in range(2):
            bsum[h, :, g] = (part[h, g, :, core].astype(F32) + bcore[h, g].astype(F32)).astype(BF16)
        across = [trade(bsum.at[h, (xc + d) % 4], brecv.at[h, d - 1], at_x(d), brecv.at[h, d - 1]) for d in (2, 1, 3)]
        yield "b_core"
        land(across)
        both = bsum[h, xc].astype(F32)
        for d in range(3):
            both = both + brecv[h, d].astype(F32)
        hid[h, xc, core] = (gelu(both[0]) * both[1]).astype(BF16)
        own = hid.at[h, xc, core]
        across = {d: trade(own, own, at_x(d), hid.at[h, (xc + 4 - d) % 4, core]) for d in (2, 1, 3)}
        cores = [trade(own, own, core_mate, hid.at[h, xc, 1 - core])]
        yield "b_x"
        for d in (1, 3, 2):
            land([across[d]])
            j = (xc + 4 - d) % 4
            cores.append(trade(hid.at[h, j, core], hid.at[h, j, core], core_mate, hid.at[h, j, 1 - core]))
        yield "c_x"
        land(cores)

        fetched(3)
        dpart[h] = dot(flat(hid[h], 576), down_ref[...]).reshape(4, 2, 24, 576).astype(BF16)
        copies = reduce_start(dpart.at[h], dnear.at[h], h)
        yield "d_dot"
        copies = far_start(dpart.at[h], dnear.at[h], copies, dsum.at[h], dfar.at[h])
        yield "d_near"
        acts[h, r, yl] = far_sum(copies, dsum.at[h], dfar.at[h]).astype(BF16)
        copies = spread_start(acts.at[h], h)
        yield "d_far"
        land(copies)

        fetched(4, 5)
        fpart[h, 0], fpart[h, 1] = split(dot(flat(acts[h], 576), enc_ref[...]))
        copies = scatter_start(fpart.at[h], frecv.at[h])
        yield "e_near"
        bias = jnp.where(mp == 0, ebias_ref[:, :128], ebias_ref[:, 128:])
        pre = scatter_sum(copies, fpart.at[h], frecv.at[h]) + bias
        codes[h, mp, tok] = jnp.maximum(pre, 0.0).astype(BF16)
        copies = gather_start(codes.at[h])
        yield "f_rs"
        land(copies)

        fetched(6, 7)
        gpart[h] = dot(join(codes[h]), dect_ref[...], 1, 1).reshape(4, 2, 24, 576).astype(BF16)
        copies = reduce_start(gpart.at[h], gnear.at[h], h)
        yield "f_ag"
        copies = far_start(gpart.at[h], gnear.at[h], copies, gsum.at[h], gfar.at[h])
        yield "g_near"
        error = far_sum(copies, gsum.at[h], gfar.at[h]) + dbias_ref[...] - acts[h, r, yl].astype(F32)
        err[h, r, yl] = error.astype(BF16)
        copies = spread_start(err.at[h], h)
        yield "g_far"
        land(copies)

        ipart[h, 0], ipart[h, 1] = split(dot(flat(err[h], 576), dect_ref[...]))
        copies = scatter_start(ipart.at[h], irecv.at[h])
        yield "h_near"
        lgrad[h, mp, tok] = scatter_sum(copies, ipart.at[h], irecv.at[h]).astype(BF16)
        copies = gather_start(lgrad.at[h])
        yield "i_rs"
        if h == 0:
            gradt_ref[...] = dot(flat(err[0], 576), join(codes[0]), 0, 0)
        else:
            gradt_ref[...] += dot(flat(err[1], 576), join(codes[1]), 0, 0)
            rows = err[k % 2, r, k // 2].astype(F32)
            err_ref[...] = jnp.where(yl == 0, rows[0:12], rows[12:24])
        yield "grad"
        land(copies)
        for c in range(2):
            for j in range(8):
                first = 24 * (4 * (2 * (j % 2) + h) + j // 2)
                lat_ref[first : first + 24, 128 * c : 128 * c + 128] = lgrad[h, c, j].astype(F32)

    fetched(0)
    pl.semaphore_wait(barrier, len(peers))

    land([trade(x_ref, xpair, y_mate, xpair)])
    mine, theirs = x_ref[...].astype(F32), xpair[...].astype(F32)
    first = jnp.where(yl == 0, mine, theirs)
    second = jnp.where(yl == 0, theirs, mine)
    xall[r, k // 2, k % 2] = jnp.concatenate([first, second], axis=0).astype(BF16)
    gather_inputs(xall)
    for at in itertools.zip_longest(chain(0), chain(1)):
        pass
    finish()


def body(inputs, gate_w, up_w, down_w, enc_w, enc_bias, dec_w, dec_bias):
    vmem = pl.BlockSpec(memory_space=pltpu.VMEM)
    reduce_scratch = [
        pltpu.VMEM((2, 4, 2, 24, 576), BF16), pltpu.VMEM((2, 7, 24, 576), BF16), pltpu.VMEM((2, 24, 576), BF16),
        pltpu.VMEM((2, 3, 24, 576), BF16), pltpu.VMEM((2, 4, 2, 24, 576), BF16),
    ]
    q_scratch = [
        pltpu.VMEM((2, 2, 8, 24, 128), BF16), pltpu.VMEM((2, 15, 24, 128), BF16), pltpu.VMEM((2, 2, 8, 24, 128), BF16)
    ]
    err, gradt, lat = pl.pallas_call(
        kernel,
        out_shape=(
            jax.ShapeDtypeStruct((12, 576), F32),
            jax.ShapeDtypeStruct((576, 256), F32),
            jax.ShapeDtypeStruct((384, 256), F32),
        ),
        in_specs=[pl.BlockSpec(memory_space=pl.ANY)] * 8,
        out_specs=(vmem, vmem, vmem),
        scratch_shapes=[
            pltpu.VMEM((12, 576), BF16), pltpu.VMEM((576, 576), BF16), pltpu.VMEM((576, 576), BF16),
            pltpu.VMEM((576, 576), BF16), pltpu.VMEM((576, 256), BF16), pltpu.VMEM((1, 256), F32),
            pltpu.VMEM((576, 256), BF16), pltpu.VMEM((1, 576), F32),
            pltpu.VMEM((12, 576), BF16), pltpu.VMEM((4, 2, 2, 24, 576), BF16),
            pltpu.VMEM((2, 2, 4, 2, 24, 576), BF16), pltpu.VMEM((2, 2, 4, 24, 576), BF16), pltpu.VMEM((2, 4, 2, 24, 576), BF16),
            pltpu.VMEM((2, 3, 2, 24, 576), BF16), pltpu.VMEM((2, 4, 2, 24, 576), BF16),
            *reduce_scratch, *reduce_scratch, *q_scratch, *q_scratch,
            pltpu.SemaphoreType.DMA((240,)), pltpu.SemaphoreType.DMA((240,)), pltpu.SemaphoreType.DMA((8,)),
        ],
        compiler_params=pltpu.CompilerParams(collective_id=0, has_side_effects=True, vmem_limit_bytes=56 << 20),
        name="step",
    )(
        inputs[0], gate_w[0], up_w[0], down_w[0], enc_w[0], enc_bias[None], dec_w[:, 0, :].T, dec_bias,
    )
    return err[None], gradt.T[:, None, :], lat


def solution(mesh):
    in_specs = (
        P("mp", "lat", "tok"),
        P("mp", "tok", "lat"),
        P("mp", "tok", "lat"),
        P("mp", "lat", "tok"),
        P("mp", "tok", "lat"),
        P("lat"),
        P("lat", "mp", "tok"),
        P("mp", "tok"),
    )
    out_specs = (P("mp", "lat", "tok"), P("lat", "mp", "tok"), P(None, "lat"))
    return jax.shard_map(body, mesh=mesh, in_specs=in_specs, out_specs=out_specs, check_vma=False)
```

```python
import itertools

import jax
import jax.numpy as jnp
from jax import lax
from jax.experimental import pallas as pl
from jax.experimental.pallas import tpu as pltpu
from jax.sharding import PartitionSpec as P

MESH = pl.DeviceIdType.MESH
F32, BF16 = jnp.float32, jnp.bfloat16
GELU = 0.7978845608028654


def dot(a, b, ca=1, cb=0):
    return lax.dot_general(a, b, (((ca,), (cb,)), ((), ())), preferred_element_type=F32)


def gelu(v):
    return 0.5 * v * (1.0 + jnp.tanh(GELU * (v + 0.044715 * v * v * v)))


def kernel(
    x_hbm, gate_hbm, up_hbm, down_hbm, enc_hbm, ebias_hbm, dect_hbm, dbias_hbm,
    err_ref, gradt_ref, lat_ref,
    x_ref, gate_ref, up_ref, down_ref, enc_ref, ebias_ref, dect_ref, dbias_ref,
    xpair, xall,
    part, bcore, bsum, brecv, hid,
    dpart, dnear, dsum, dfar, acts,
    gpart, gnear, gsum, gfar, err,
    fpart, frecv, codes, ipart, irecv, lgrad,
    ssem, rsem, lsem,
):
    mp, tok, lat = lax.axis_index("mp"), lax.axis_index("tok"), lax.axis_index("lat")
    z, yl = lat // 2, lat % 2
    r, k = z % 4, z // 4
    xc, core = tok // 2, tok % 2
    q = mp * 8 + tok

    known = {}

    def at_z(d, y):
        if ("z", d % 16) not in known:
            known["z", d % 16] = ((z + d + 16) % 16) * 2
        return (mp, tok, known["z", d % 16] + y)

    def at_x(d):
        if ("x", d) not in known:
            known["x", d] = ((xc + d) % 4) * 2 + core
        return (mp, known["x", d], lat)

    def index_q(d):
        if ("q", d % 16) not in known:
            o = (q + d + 16) % 16
            known["q", d % 16] = (o // 8, o % 8)
        return known["q", d % 16]

    def at_q(d):
        return (*index_q(d), lat)

    y_mate = (mp, tok, z * 2 + 1 - yl)
    core_mate = (mp, xc * 2 + 1 - core, lat)

    barrier = pltpu.get_barrier_semaphore()
    peers = [at_z(d, y) for d in (8, 4, 12, 2, -2, 1, -1) for y in range(2)]
    peers += [y_mate] + [at_q(d) for d in range(1, 16)]
    for peer in peers:
        pl.semaphore_signal(barrier, inc=1, device_id=peer, device_id_type=MESH)

    fetches = [
        pltpu.make_async_copy(src, dst, lsem.at[i])
        for i, (src, dst) in enumerate(
            (
                (x_hbm, x_ref), (gate_hbm, gate_ref), (up_hbm, up_ref), (down_hbm, down_ref),
                (enc_hbm, enc_ref), (ebias_hbm, ebias_ref), (dect_hbm, dect_ref), (dbias_hbm, dbias_ref),
            )
        )
    ]
    for fetch in fetches:
        fetch.start()

    count = [0]
    sent, awaited, landed, here = [], [], set(), set()

    def slots(n):
        count[0] += n
        return count[0] - n

    def send(src, dst, peer, out, into):
        copy = pltpu.make_async_remote_copy(
            src_ref=src, dst_ref=dst, send_sem=ssem.at[out], recv_sem=rsem.at[into], device_id=peer, device_id_type=MESH
        )
        copy.start()
        sent.append(copy)

    def coming(landing, slot):
        copy = pltpu.make_async_remote_copy(
            src_ref=landing, dst_ref=landing, send_sem=ssem.at[slot], recv_sem=rsem.at[slot], device_id=y_mate, device_id_type=MESH
        )
        awaited.append(copy)
        return copy

    def trade(src, dst, peer, landing):
        slot = slots(1)
        send(src, dst, peer, slot, slot)
        return coming(landing, slot)

    def land(copies):
        for copy in copies:
            landed.add(id(copy))
            copy.wait_recv()

    def fetched(*numbers):
        for i in numbers:
            if i not in here:
                here.add(i)
                fetches[i].wait()

    def finish():
        land([copy for copy in awaited if id(copy) not in landed])
        fetched(*range(len(fetches)))
        for copy in sent:
            copy.wait_send()

    def flat(v, width):
        return v.astype(F32).reshape(192, width).astype(BF16)

    def gather_inputs(buf):
        up1, down1, two = slots(4), slots(4), slots(4)
        far = {}
        for off in (2, 3, 1):
            c = (k + 4 - off) % 4
            own = buf.at[r, k // 2, k % 2]
            far[off] = trade(own, own, at_z(4 * off, yl), buf.at[r, c // 2, c % 2])
        for off in (0, 3, 1, 2):
            c = (k + 4 - off) % 4
            if off:
                land([far[off]])
            piece = buf.at[r, c // 2, c % 2]
            send(piece, piece, (mp, tok, ((z + 18 - 4 * (c // 2)) % 16) * 2 + yl), two + c, two + c)
            send(piece, piece, at_z(1, yl), up1 + c, up1 + c)
            send(piece, piece, at_z(-1, yl), down1 + c, down1 + c)
        for c in range(4):
            land([
                coming(buf.at[(r + 3) % 4, c // 2, c % 2], up1 + c),
                coming(buf.at[(r + 1) % 4, c // 2, c % 2], down1 + c),
                coming(buf.at[(r + 2) % 4, c // 2, c % 2], two + c),
            ])

    def reduce_start(p, near, h):
        base = slots(7)
        for i, step in enumerate((2, 1, -1)):
            for o in range(2):
                d = step if i else (2 if o == h else -2)
                y = yl if o == 0 else 1 - yl
                s = 2 * i + o
                send(p.at[(r + d + 4) % 4, y], near.at[s], at_z(d, y), base + s, base + s)
        send(p.at[r, 1 - yl], near.at[6], y_mate, base + 6, base + 6)
        return [coming(near.at[s], base + s) for s in range(7)]

    def far_start(p, near, copies, total, far):
        land(copies)
        acc = p[r, yl].astype(F32)
        for s in range(7):
            acc = acc + near[s].astype(F32)
        total[...] = acc.astype(BF16)
        return [trade(total, far.at[off - 1], at_z(4 * off, yl), far.at[off - 1]) for off in (2, 1, 3)]

    def far_sum(copies, total, far):
        land(copies)
        return total[...].astype(F32) + far[0].astype(F32) + far[1].astype(F32) + far[2].astype(F32)

    def spread_start(buf, h):
        base = slots(6)
        own = buf.at[r, yl]
        copies = []
        for i, step in enumerate((2, 1, -1)):
            for o in range(2):
                d = step if i else (-2 if o == h else 2)
                y = yl if o == 0 else 1 - yl
                s = base + 2 * i + o
                send(own, own, at_z(d, y), s, s)
                copies.append(coming(buf.at[(r - d + 4) % 4, y], s))
        return copies + [trade(own, own, y_mate, buf.at[r, 1 - yl])]

    def scatter_start(p, recv):
        copies = []
        for d in range(1, 16):
            copies.append(trade(p.at[index_q(d)], recv.at[d - 1], at_q(d), recv.at[d - 1]))
        return copies

    def scatter_sum(copies, p, recv):
        acc = p[mp, tok].astype(F32)
        for d, copy in enumerate(copies):
            land([copy])
            acc = acc + recv[d].astype(F32)
        return acc

    def gather_start(buf):
        own = buf.at[mp, tok]
        copies = []
        for d in range(1, 16):
            copies.append(trade(own, own, at_q(d), buf.at[index_q(-d)]))
        return copies

    def split(v):
        v = v.reshape(8, 24, 256)
        return v[:, :, :128].astype(BF16), v[:, :, 128:].astype(BF16)

    def join(buf):
        return jnp.concatenate([flat(buf[0], 128), flat(buf[1], 128)], axis=1)

    def chain(h):
        block = flat(xall[:, :, h], 576)
        fetched(1)
        part[h, 0] = dot(block, gate_ref[...]).reshape(4, 2, 24, 576).astype(BF16)
        cores = [trade(part.at[h, 0, :, 1 - core], bcore.at[h, 0], core_mate, bcore.at[h, 0])]
        fetched(2)
        part[h, 1] = dot(block, up_ref[...]).reshape(4, 2, 24, 576).astype(BF16)
        cores += [trade(part.at[h, 1, :, 1 - core], bcore.at[h, 1], core_mate, bcore.at[h, 1])]
        yield "b_dot"
        land(cores)
        for g in range(2):
            bsum[h, :, g] = (part[h, g, :, core].astype(F32) + bcore[h, g].astype(F32)).astype(BF16)
        across = [trade(bsum.at[h, (xc + d) % 4], brecv.at[h, d - 1], at_x(d), brecv.at[h, d - 1]) for d in (2, 1, 3)]
        yield "b_core"
        land(across)
        both = bsum[h, xc].astype(F32)
        for d in range(3):
            both = both + brecv[h, d].astype(F32)
        hid[h, xc, core] = (gelu(both[0]) * both[1]).astype(BF16)
        own = hid.at[h, xc, core]
        across = {d: trade(own, own, at_x(d), hid.at[h, (xc + 4 - d) % 4, core]) for d in (2, 1, 3)}
        cores = [trade(own, own, core_mate, hid.at[h, xc, 1 - core])]
        yield "b_x"
        for d in (1, 3, 2):
            land([across[d]])
            j = (xc + 4 - d) % 4
            cores.append(trade(hid.at[h, j, core], hid.at[h, j, core], core_mate, hid.at[h, j, 1 - core]))
        land(cores)

        fetched(3)
        dpart[h] = dot(flat(hid[h], 576), down_ref[...]).reshape(4, 2, 24, 576).astype(BF16)
        copies = reduce_start(dpart.at[h], dnear.at[h], h)
        yield "d_dot"
        copies = far_start(dpart.at[h], dnear.at[h], copies, dsum.at[h], dfar.at[h])
        yield "d_near"
        acts[h, r, yl] = far_sum(copies, dsum.at[h], dfar.at[h]).astype(BF16)
        copies = spread_start(acts.at[h], h)
        yield "d_far"
        land(copies)

        fetched(4, 5)
        fpart[h, 0], fpart[h, 1] = split(dot(flat(acts[h], 576), enc_ref[...]))
        copies = scatter_start(fpart.at[h], frecv.at[h])
        yield "e_near"
        bias = jnp.where(mp == 0, ebias_ref[:, :128], ebias_ref[:, 128:])
        pre = scatter_sum(copies, fpart.at[h], frecv.at[h]) + bias
        codes[h, mp, tok] = jnp.maximum(pre, 0.0).astype(BF16)
        copies = gather_start(codes.at[h])
        yield "f_rs"
        land(copies)

        fetched(6, 7)
        gpart[h] = dot(join(codes[h]), dect_ref[...], 1, 1).reshape(4, 2, 24, 576).astype(BF16)
        copies = reduce_start(gpart.at[h], gnear.at[h], h)
        yield "f_ag"
        copies = far_start(gpart.at[h], gnear.at[h], copies, gsum.at[h], gfar.at[h])
        yield "g_near"
        error = far_sum(copies, gsum.at[h], gfar.at[h]) + dbias_ref[...] - acts[h, r, yl].astype(F32)
        err[h, r, yl] = error.astype(BF16)
        copies = spread_start(err.at[h], h)
        yield "g_far"
        land(copies)

        ipart[h, 0], ipart[h, 1] = split(dot(flat(err[h], 576), dect_ref[...]))
        copies = scatter_start(ipart.at[h], irecv.at[h])
        yield "h_near"
        lgrad[h, mp, tok] = scatter_sum(copies, ipart.at[h], irecv.at[h]).astype(BF16)
        copies = gather_start(lgrad.at[h])
        yield "i_rs"
        if h == 0:
            gradt_ref[...] = dot(flat(err[0], 576), join(codes[0]), 0, 0)
        else:
            gradt_ref[...] += dot(flat(err[1], 576), join(codes[1]), 0, 0)
            rows = err[k % 2, r, k // 2].astype(F32)
            err_ref[...] = jnp.where(yl == 0, rows[0:12], rows[12:24])
        yield "grad"
        land(copies)
        for c in range(2):
            for j in range(8):
                first = 24 * (4 * (2 * (j % 2) + h) + j // 2)
                lat_ref[first : first + 24, 128 * c : 128 * c + 128] = lgrad[h, c, j].astype(F32)

    fetched(0)
    pl.semaphore_wait(barrier, len(peers))

    land([trade(x_ref, xpair, y_mate, xpair)])
    mine, theirs = x_ref[...].astype(F32), xpair[...].astype(F32)
    first = jnp.where(yl == 0, mine, theirs)
    second = jnp.where(yl == 0, theirs, mine)
    xall[r, k // 2, k % 2] = jnp.concatenate([first, second], axis=0).astype(BF16)
    gather_inputs(xall)
    for at in itertools.zip_longest(chain(0), chain(1)):
        pass
    finish()


def body(inputs, gate_w, up_w, down_w, enc_w, enc_bias, dec_w, dec_bias):
    vmem = pl.BlockSpec(memory_space=pltpu.VMEM)
    reduce_scratch = [
        pltpu.VMEM((2, 4, 2, 24, 576), BF16), pltpu.VMEM((2, 7, 24, 576), BF16), pltpu.VMEM((2, 24, 576), BF16),
        pltpu.VMEM((2, 3, 24, 576), BF16), pltpu.VMEM((2, 4, 2, 24, 576), BF16),
    ]
    q_scratch = [
        pltpu.VMEM((2, 2, 8, 24, 128), BF16), pltpu.VMEM((2, 15, 24, 128), BF16), pltpu.VMEM((2, 2, 8, 24, 128), BF16)
    ]
    operands = (inputs[0], gate_w[0], up_w[0], down_w[0], enc_w[0], enc_bias[None], dec_w[:, 0, :].T, dec_bias)
    err, gradt, lat = pl.pallas_call(
        kernel,
        out_shape=(
            jax.ShapeDtypeStruct((12, 576), F32),
            jax.ShapeDtypeStruct((576, 256), F32),
            jax.ShapeDtypeStruct((384, 256), F32),
        ),
        in_specs=[pl.BlockSpec(memory_space=pl.ANY)] * 8,
        out_specs=(vmem, vmem, vmem),
        scratch_shapes=[
            pltpu.VMEM((12, 576), BF16), pltpu.VMEM((576, 576), BF16), pltpu.VMEM((576, 576), BF16), pltpu.VMEM((576, 576), BF16),
            pltpu.VMEM((576, 256), BF16), pltpu.VMEM((1, 256), F32),
            pltpu.VMEM((576, 256), BF16), pltpu.VMEM((1, 576), F32),
            pltpu.VMEM((12, 576), BF16), pltpu.VMEM((4, 2, 2, 24, 576), BF16),
            pltpu.VMEM((2, 2, 4, 2, 24, 576), BF16), pltpu.VMEM((2, 2, 4, 24, 576), BF16), pltpu.VMEM((2, 4, 2, 24, 576), BF16),
            pltpu.VMEM((2, 3, 2, 24, 576), BF16), pltpu.VMEM((2, 4, 2, 24, 576), BF16),
            *reduce_scratch, *reduce_scratch, *q_scratch, *q_scratch,
            pltpu.SemaphoreType.DMA((240,)), pltpu.SemaphoreType.DMA((240,)), pltpu.SemaphoreType.DMA((8,)),
        ],
        compiler_params=pltpu.CompilerParams(collective_id=0, has_side_effects=True, vmem_limit_bytes=40 << 20),
        name="step",
    )(
        *(pltpu.with_memory_space_constraint(v, pltpu.HBM) for v in operands)
    )
    return err[None], gradt.T[:, None, :], lat


def solution(mesh):
    in_specs = (
        P("mp", "lat", "tok"),
        P("mp", "tok", "lat"),
        P("mp", "tok", "lat"),
        P("mp", "lat", "tok"),
        P("mp", "tok", "lat"),
        P("lat"),
        P("lat", "mp", "tok"),
        P("mp", "tok"),
    )
    out_specs = (P("mp", "lat", "tok"), P("lat", "mp", "tok"), P(None, "lat"))
    return jax.shard_map(body, mesh=mesh, in_specs=in_specs, out_specs=out_specs, check_vma=False)
```

```python
import itertools

import jax
import jax.numpy as jnp
from jax import lax
from jax.experimental import pallas as pl
from jax.experimental.pallas import tpu as pltpu
from jax.sharding import PartitionSpec as P

MESH = pl.DeviceIdType.MESH
F32, BF16 = jnp.float32, jnp.bfloat16
GELU = 0.7978845608028654


def dot(a, b, ca=1, cb=0):
    return lax.dot_general(a, b, (((ca,), (cb,)), ((), ())), preferred_element_type=F32)


def gelu(v):
    return 0.5 * v * (1.0 + jnp.tanh(GELU * (v + 0.044715 * v * v * v)))


def kernel(
    x_hbm, gate_hbm, up_hbm, down_hbm, enc_hbm, ebias_hbm, dect_hbm, dbias_hbm,
    err_ref, gradt_ref, lat_ref,
    gate_ref, up_ref, down_ref, enc_ref, ebias_ref, dect_ref, dbias_ref,
    xall,
    part, bcore, bsum, brecv, hid,
    dpart, dnear, dsum, dfar, acts,
    gpart, gnear, gsum, gfar, err,
    fpart, frecv, codes, ipart, irecv, lgrad,
    ssem, rsem, lsem,
):
    mp, tok, lat = lax.axis_index("mp"), lax.axis_index("tok"), lax.axis_index("lat")
    z, yl = lat // 2, lat % 2
    r, k = z % 4, z // 4
    xc, core = tok // 2, tok % 2
    q = mp * 8 + tok

    known = {}

    def at_z(d, y):
        if ("z", d % 16) not in known:
            known["z", d % 16] = ((z + d + 16) % 16) * 2
        return (mp, tok, known["z", d % 16] + y)

    def at_x(d):
        if ("x", d) not in known:
            known["x", d] = ((xc + d) % 4) * 2 + core
        return (mp, known["x", d], lat)

    def index_q(d):
        if ("q", d % 16) not in known:
            o = (q + d + 16) % 16
            known["q", d % 16] = (o // 8, o % 8)
        return known["q", d % 16]

    def at_q(d):
        return (*index_q(d), lat)

    y_mate = (mp, tok, z * 2 + 1 - yl)
    core_mate = (mp, xc * 2 + 1 - core, lat)

    barrier = pltpu.get_barrier_semaphore()
    peers = [at_z(d, y) for d in (4, -4, 2, -2, 1, -1) for y in range(2)]
    peers += [y_mate] + [at_q(d) for d in range(1, 16)]
    for peer in peers:
        pl.semaphore_signal(barrier, inc=1, device_id=peer, device_id_type=MESH)

    fetches = [
        pltpu.make_async_copy(src, dst, lsem.at[i])
        for i, (src, dst) in enumerate(
            (
                (x_hbm, xall.at[r, k // 2, k % 2, yl]), (gate_hbm, gate_ref), (up_hbm, up_ref), (down_hbm, down_ref),
                (enc_hbm, enc_ref), (ebias_hbm, ebias_ref), (dect_hbm, dect_ref), (dbias_hbm, dbias_ref),
            )
        )
    ]
    for fetch in fetches:
        fetch.start()

    count = [0]
    sent, awaited, landed, here = [], [], set(), set()

    def slots(n):
        count[0] += n
        return count[0] - n

    def send(src, dst, peer, out, into):
        copy = pltpu.make_async_remote_copy(
            src_ref=src, dst_ref=dst, send_sem=ssem.at[out], recv_sem=rsem.at[into], device_id=peer, device_id_type=MESH
        )
        copy.start()
        sent.append(copy)

    def coming(landing, slot):
        copy = pltpu.make_async_remote_copy(
            src_ref=landing, dst_ref=landing, send_sem=ssem.at[slot], recv_sem=rsem.at[slot], device_id=y_mate, device_id_type=MESH
        )
        awaited.append(copy)
        return copy

    def trade(src, dst, peer, landing):
        slot = slots(1)
        send(src, dst, peer, slot, slot)
        return coming(landing, slot)

    def land(copies):
        for copy in copies:
            landed.add(id(copy))
            copy.wait_recv()

    def fetched(*numbers):
        for i in numbers:
            if i not in here:
                here.add(i)
                fetches[i].wait()

    def finish():
        land([copy for copy in awaited if id(copy) not in landed])
        fetched(*range(len(fetches)))
        for copy in sent:
            copy.wait_send()

    def flat(v, width):
        return v.astype(F32).reshape(192, width).astype(BF16)

    def gather_inputs(buf):
        base, up1, down1, two = slots(7), slots(4), slots(4), slots(4)
        own = buf.at[r, k // 2, k % 2, yl]

        def chunk(off):
            c = (k + 4 - off) % 4
            return c, buf.at[r, c // 2, c % 2]

        def pass_on(off):
            c, piece = chunk(off)
            send(piece, piece, (mp, tok, ((z + 18 - 4 * (c // 2)) % 16) * 2 + yl), two + c, two + c)
            send(piece, piece, at_z(1, yl), up1 + c, up1 + c)
            send(piece, piece, at_z(-1, yl), down1 + c, down1 + c)

        for i, d in enumerate((4, -4)):
            for y in range(2):
                send(own, own, at_z(d, y), base + 2 * i + y, base + 2 * i + yl)
        send(own, own, y_mate, base + 4, base + 4)
        for i, off in enumerate((1, 3)):
            land([coming(chunk(off)[1].at[y], base + 2 * i + y) for y in range(2)])
        c = (k + 3 + 2 * core) % 4
        relay = buf.at[r, c // 2, c % 2]
        send(relay, relay, (mp, tok, ((z + 20 - 8 * core) % 16) * 2 + yl), base + 5, base + 5)
        land([coming(chunk(0)[1].at[1 - yl], base + 4)])
        pass_on(0)
        pass_on(1)
        pass_on(3)
        land([coming(chunk(2)[1], base + 5)])
        pass_on(2)
        for c in range(4):
            land([
                coming(buf.at[(r + 3) % 4, c // 2, c % 2], up1 + c),
                coming(buf.at[(r + 1) % 4, c // 2, c % 2], down1 + c),
                coming(buf.at[(r + 2) % 4, c // 2, c % 2], two + c),
            ])

    def reduce_start(p, near, h):
        base = slots(7)
        for i, step in enumerate((2, 1, -1)):
            for o in range(2):
                d = step if i else (2 if o == h else -2)
                y = yl if o == 0 else 1 - yl
                s = 2 * i + o
                send(p.at[(r + d + 4) % 4, y], near.at[s], at_z(d, y), base + s, base + s)
        send(p.at[r, 1 - yl], near.at[6], y_mate, base + 6, base + 6)
        return [coming(near.at[s], base + s) for s in range(7)]

    def far_start(p, near, copies, total, far):
        land(copies)
        acc = p[r, yl].astype(F32)
        for s in range(7):
            acc = acc + near[s].astype(F32)
        total[...] = acc.astype(BF16)
        return [trade(total, far.at[off - 1], at_z(4 * off, yl), far.at[off - 1]) for off in (2, 1, 3)]

    def far_sum(copies, total, far):
        land(copies)
        return total[...].astype(F32) + far[0].astype(F32) + far[1].astype(F32) + far[2].astype(F32)

    def spread_start(buf, h):
        base = slots(6)
        own = buf.at[r, yl]
        copies = []
        for i, step in enumerate((2, 1, -1)):
            for o in range(2):
                d = step if i else (-2 if o == h else 2)
                y = yl if o == 0 else 1 - yl
                s = base + 2 * i + o
                send(own, own, at_z(d, y), s, s)
                copies.append(coming(buf.at[(r - d + 4) % 4, y], s))
        return copies + [trade(own, own, y_mate, buf.at[r, 1 - yl])]

    def scatter_start(p, recv):
        copies = []
        for d in range(1, 16):
            copies.append(trade(p.at[index_q(d)], recv.at[d - 1], at_q(d), recv.at[d - 1]))
        return copies

    def scatter_sum(copies, p, recv):
        acc = p[mp, tok].astype(F32)
        for d, copy in enumerate(copies):
            land([copy])
            acc = acc + recv[d].astype(F32)
        return acc

    def gather_start(buf):
        own = buf.at[mp, tok]
        copies = []
        for d in range(1, 16):
            copies.append(trade(own, own, at_q(d), buf.at[index_q(-d)]))
        return copies

    def split(v):
        v = v.reshape(8, 24, 256)
        return v[:, :, :128].astype(BF16), v[:, :, 128:].astype(BF16)

    def join(buf):
        return jnp.concatenate([flat(buf[0], 128), flat(buf[1], 128)], axis=1)

    def chain(h):
        pieces = [
            jnp.concatenate([xall[i // 2, i % 2, h, y].astype(F32) for y in range(2)], axis=0) for i in range(8)
        ]
        block = jnp.concatenate(pieces, axis=0).astype(BF16)
        fetched(1)
        part[h, 0] = dot(block, gate_ref[...]).reshape(4, 2, 24, 576).astype(BF16)
        cores = [trade(part.at[h, 0, :, 1 - core], bcore.at[h, 0], core_mate, bcore.at[h, 0])]
        fetched(2)
        part[h, 1] = dot(block, up_ref[...]).reshape(4, 2, 24, 576).astype(BF16)
        cores += [trade(part.at[h, 1, :, 1 - core], bcore.at[h, 1], core_mate, bcore.at[h, 1])]
        yield "b_dot"
        land(cores)
        for g in range(2):
            bsum[h, :, g] = (part[h, g, :, core].astype(F32) + bcore[h, g].astype(F32)).astype(BF16)
        across = [trade(bsum.at[h, (xc + d) % 4], brecv.at[h, d - 1], at_x(d), brecv.at[h, d - 1]) for d in (2, 1, 3)]
        yield "b_core"
        land(across)
        both = bsum[h, xc].astype(F32)
        for d in range(3):
            both = both + brecv[h, d].astype(F32)
        hid[h, xc, core] = (gelu(both[0]) * both[1]).astype(BF16)
        own = hid.at[h, xc, core]
        across = {d: trade(own, own, at_x(d), hid.at[h, (xc + 4 - d) % 4, core]) for d in (2, 1, 3)}
        cores = [trade(own, own, core_mate, hid.at[h, xc, 1 - core])]
        yield "b_x"
        for d in (1, 3, 2):
            land([across[d]])
            j = (xc + 4 - d) % 4
            cores.append(trade(hid.at[h, j, core], hid.at[h, j, core], core_mate, hid.at[h, j, 1 - core]))
        land(cores)

        fetched(3)
        dpart[h] = dot(flat(hid[h], 576), down_ref[...]).reshape(4, 2, 24, 576).astype(BF16)
        copies = reduce_start(dpart.at[h], dnear.at[h], h)
        yield "d_dot"
        copies = far_start(dpart.at[h], dnear.at[h], copies, dsum.at[h], dfar.at[h])
        yield "d_near"
        acts[h, r, yl] = far_sum(copies, dsum.at[h], dfar.at[h]).astype(BF16)
        copies = spread_start(acts.at[h], h)
        yield "d_far"
        land(copies)

        fetched(4, 5)
        fpart[h, 0], fpart[h, 1] = split(dot(flat(acts[h], 576), enc_ref[...]))
        copies = scatter_start(fpart.at[h], frecv.at[h])
        yield "e_near"
        bias = jnp.where(mp == 0, ebias_ref[:, :128], ebias_ref[:, 128:])
        pre = scatter_sum(copies, fpart.at[h], frecv.at[h]) + bias
        codes[h, mp, tok] = jnp.maximum(pre, 0.0).astype(BF16)
        copies = gather_start(codes.at[h])
        yield "f_rs"
        land(copies)

        fetched(6, 7)
        gpart[h] = dot(join(codes[h]), dect_ref[...], 1, 1).reshape(4, 2, 24, 576).astype(BF16)
        copies = reduce_start(gpart.at[h], gnear.at[h], h)
        yield "f_ag"
        copies = far_start(gpart.at[h], gnear.at[h], copies, gsum.at[h], gfar.at[h])
        yield "g_near"
        error = far_sum(copies, gsum.at[h], gfar.at[h]) + dbias_ref[...] - acts[h, r, yl].astype(F32)
        err[h, r, yl] = error.astype(BF16)
        copies = spread_start(err.at[h], h)
        yield "g_far"
        land(copies)

        ipart[h, 0], ipart[h, 1] = split(dot(flat(err[h], 576), dect_ref[...]))
        copies = scatter_start(ipart.at[h], irecv.at[h])
        yield "h_near"
        lgrad[h, mp, tok] = scatter_sum(copies, ipart.at[h], irecv.at[h]).astype(BF16)
        copies = gather_start(lgrad.at[h])
        yield "i_rs"
        if h == 0:
            gradt_ref[...] = dot(flat(err[0], 576), join(codes[0]), 0, 0)
        else:
            gradt_ref[...] += dot(flat(err[1], 576), join(codes[1]), 0, 0)
            rows = err[k % 2, r, k // 2].astype(F32)
            err_ref[...] = jnp.where(yl == 0, rows[0:12], rows[12:24])
        yield "grad"
        land(copies)
        for c in range(2):
            for j in range(8):
                first = 24 * (4 * (2 * (j % 2) + h) + j // 2)
                lat_ref[first : first + 24, 128 * c : 128 * c + 128] = lgrad[h, c, j].astype(F32)

    fetched(0)
    pl.semaphore_wait(barrier, len(peers))

    gather_inputs(xall)
    for at in itertools.zip_longest(chain(0), chain(1)):
        pass
    finish()


def body(inputs, gate_w, up_w, down_w, enc_w, enc_bias, dec_w, dec_bias):
    vmem = pl.BlockSpec(memory_space=pltpu.VMEM)
    reduce_scratch = [
        pltpu.VMEM((2, 4, 2, 24, 576), BF16), pltpu.VMEM((2, 7, 24, 576), BF16), pltpu.VMEM((2, 24, 576), BF16),
        pltpu.VMEM((2, 3, 24, 576), BF16), pltpu.VMEM((2, 4, 2, 24, 576), BF16),
    ]
    q_scratch = [
        pltpu.VMEM((2, 2, 8, 24, 128), BF16), pltpu.VMEM((2, 15, 24, 128), BF16), pltpu.VMEM((2, 2, 8, 24, 128), BF16)
    ]
    operands = (inputs[0], gate_w[0], up_w[0], down_w[0], enc_w[0], enc_bias[None], dec_w[:, 0, :].T, dec_bias)
    err, gradt, lat = pl.pallas_call(
        kernel,
        out_shape=(
            jax.ShapeDtypeStruct((12, 576), F32),
            jax.ShapeDtypeStruct((576, 256), F32),
            jax.ShapeDtypeStruct((384, 256), F32),
        ),
        in_specs=[pl.BlockSpec(memory_space=pl.ANY)] * 8,
        out_specs=(vmem, vmem, vmem),
        scratch_shapes=[
            pltpu.VMEM((576, 576), BF16), pltpu.VMEM((576, 576), BF16), pltpu.VMEM((576, 576), BF16),
            pltpu.VMEM((576, 256), BF16), pltpu.VMEM((1, 256), F32),
            pltpu.VMEM((576, 256), BF16), pltpu.VMEM((1, 576), F32),
            pltpu.VMEM((4, 2, 2, 2, 12, 576), BF16),
            pltpu.VMEM((2, 2, 4, 2, 24, 576), BF16), pltpu.VMEM((2, 2, 4, 24, 576), BF16), pltpu.VMEM((2, 4, 2, 24, 576), BF16),
            pltpu.VMEM((2, 3, 2, 24, 576), BF16), pltpu.VMEM((2, 4, 2, 24, 576), BF16),
            *reduce_scratch, *reduce_scratch, *q_scratch, *q_scratch,
            pltpu.SemaphoreType.DMA((240,)), pltpu.SemaphoreType.DMA((240,)), pltpu.SemaphoreType.DMA((8,)),
        ],
        compiler_params=pltpu.CompilerParams(collective_id=0, has_side_effects=True, vmem_limit_bytes=40 << 20),
        name="step",
    )(
        *(pltpu.with_memory_space_constraint(v, pltpu.HBM) for v in operands)
    )
    return err[None], gradt.T[:, None, :], lat


def solution(mesh):
    in_specs = (
        P("mp", "lat", "tok"),
        P("mp", "tok", "lat"),
        P("mp", "tok", "lat"),
        P("mp", "lat", "tok"),
        P("mp", "tok", "lat"),
        P("lat"),
        P("lat", "mp", "tok"),
        P("mp", "tok"),
    )
    out_specs = (P("mp", "lat", "tok"), P("lat", "mp", "tok"), P(None, "lat"))
    return jax.shard_map(body, mesh=mesh, in_specs=in_specs, out_specs=out_specs, check_vma=False)
```

```python
import itertools

import jax
import jax.numpy as jnp
from jax import lax
from jax.experimental import pallas as pl
from jax.experimental.pallas import tpu as pltpu
from jax.sharding import PartitionSpec as P

MESH = pl.DeviceIdType.MESH
F32, BF16 = jnp.float32, jnp.bfloat16
GELU = 0.7978845608028654


def dot(a, b, ca=1, cb=0):
    return lax.dot_general(a, b, (((ca,), (cb,)), ((), ())), preferred_element_type=F32)


def gelu(v):
    return 0.5 * v * (1.0 + jnp.tanh(GELU * (v + 0.044715 * v * v * v)))


def kernel(
    x_hbm, gate_hbm, up_hbm, down_hbm, enc_hbm, ebias_hbm, dect_hbm, dbias_hbm,
    err_ref, gradt_ref, lat_ref,
    gate_ref, up_ref, down_ref, enc_ref, ebias_ref, dect_ref, dbias_ref,
    xall,
    part, bcore, bsum, brecv, hid,
    dpart, dnear, dsum, dfar, acts,
    gpart, gnear, gsum, gfar, err,
    fpart, frecv, codes, ipart, irecv, lgrad,
    ssem, rsem, lsem,
):
    mp, tok, lat = lax.axis_index("mp"), lax.axis_index("tok"), lax.axis_index("lat")
    z, yl = lat // 2, lat % 2
    r, k = z % 4, z // 4
    xc, core = tok // 2, tok % 2
    q = mp * 8 + tok

    known = {}

    def at_z(d, y):
        if ("z", d % 16) not in known:
            known["z", d % 16] = ((z + d + 16) % 16) * 2
        return (mp, tok, known["z", d % 16] + y)

    def at_x(d):
        if ("x", d) not in known:
            known["x", d] = ((xc + d) % 4) * 2 + core
        return (mp, known["x", d], lat)

    def index_q(a, d, c):
        if ("q", a, d % 4, c) not in known:
            known["q", a, d % 4, c] = (1 - mp if a else mp, ((xc + d + 4) % 4) * 2 + (1 - core if c else core))
        return known["q", a, d % 4, c]

    others = [(a, d, c) for a, d in ((1, 2), (1, 1), (1, 3), (0, 2), (1, 0), (0, 1), (0, 3), (0, 0)) for c in range(2)][:-2]
    others.append((0, 0, 1))

    y_mate = (mp, tok, z * 2 + 1 - yl)
    core_mate = (mp, xc * 2 + 1 - core, lat)

    barrier = pltpu.get_barrier_semaphore()
    peers = [at_z(d, y) for d in (4, -4, 2, -2, 1, -1) for y in range(2)]
    peers += [y_mate] + [(*index_q(*o), lat) for o in others]
    for peer in peers:
        pl.semaphore_signal(barrier, inc=1, device_id=peer, device_id_type=MESH)

    fetches = [
        pltpu.make_async_copy(src, dst, lsem.at[i])
        for i, (src, dst) in enumerate(
            (
                (x_hbm, xall.at[r, k // 2, k % 2, yl]), (gate_hbm, gate_ref), (up_hbm, up_ref), (down_hbm, down_ref),
                (enc_hbm, enc_ref), (ebias_hbm, ebias_ref), (dect_hbm, dect_ref), (dbias_hbm, dbias_ref),
            )
        )
    ]
    for fetch in fetches:
        fetch.start()

    count = [0]
    sent, awaited, landed, here = [], [], set(), set()

    def slots(n):
        count[0] += n
        return count[0] - n

    def send(src, dst, peer, out, into):
        copy = pltpu.make_async_remote_copy(
            src_ref=src, dst_ref=dst, send_sem=ssem.at[out], recv_sem=rsem.at[into], device_id=peer, device_id_type=MESH
        )
        copy.start()
        sent.append(copy)

    def coming(landing, slot):
        copy = pltpu.make_async_remote_copy(
            src_ref=landing, dst_ref=landing, send_sem=ssem.at[slot], recv_sem=rsem.at[slot], device_id=y_mate, device_id_type=MESH
        )
        awaited.append(copy)
        return copy

    def trade(src, dst, peer, landing):
        slot = slots(1)
        send(src, dst, peer, slot, slot)
        return coming(landing, slot)

    def land(copies):
        for copy in copies:
            landed.add(id(copy))
            copy.wait_recv()

    def fetched(*numbers):
        for i in numbers:
            if i not in here:
                here.add(i)
                fetches[i].wait()

    def finish():
        land([copy for copy in awaited if id(copy) not in landed])
        fetched(*range(len(fetches)))
        for copy in sent:
            copy.wait_send()

    def flat(v, width):
        return v.astype(F32).reshape(192, width).astype(BF16)

    def gather_inputs(buf):
        base, up1, down1, two = slots(7), slots(4), slots(4), slots(4)
        own = buf.at[r, k // 2, k % 2, yl]

        def chunk(off):
            c = (k + 4 - off) % 4
            return c, buf.at[r, c // 2, c % 2]

        def pass_on(off):
            c, piece = chunk(off)
            send(piece, piece, (mp, tok, ((z + 18 - 4 * (c // 2)) % 16) * 2 + yl), two + c, two + c)
            send(piece, piece, at_z(1, yl), up1 + c, up1 + c)
            send(piece, piece, at_z(-1, yl), down1 + c, down1 + c)

        for i, d in enumerate((4, -4)):
            for y in range(2):
                send(own, own, at_z(d, y), base + 2 * i + y, base + 2 * i + yl)
        send(own, own, y_mate, base + 4, base + 4)
        for i, off in enumerate((1, 3)):
            land([coming(chunk(off)[1].at[y], base + 2 * i + y) for y in range(2)])
        c = (k + 3 + 2 * core) % 4
        relay = buf.at[r, c // 2, c % 2]
        send(relay, relay, (mp, tok, ((z + 20 - 8 * core) % 16) * 2 + yl), base + 5, base + 5)
        land([coming(chunk(0)[1].at[1 - yl], base + 4)])
        pass_on(0)
        pass_on(1)
        pass_on(3)
        land([coming(chunk(2)[1], base + 5)])
        pass_on(2)
        for c in range(4):
            land([
                coming(buf.at[(r + 3) % 4, c // 2, c % 2], up1 + c),
                coming(buf.at[(r + 1) % 4, c // 2, c % 2], down1 + c),
                coming(buf.at[(r + 2) % 4, c // 2, c % 2], two + c),
            ])

    def reduce_start(p, near, h):
        base = slots(7)
        for i, step in enumerate((2, 1, -1)):
            for o in range(2):
                d = step if i else (2 if o == h else -2)
                y = yl if o == 0 else 1 - yl
                s = 2 * i + o
                send(p.at[(r + d + 4) % 4, y], near.at[s], at_z(d, y), base + s, base + s)
        send(p.at[r, 1 - yl], near.at[6], y_mate, base + 6, base + 6)
        return [coming(near.at[s], base + s) for s in range(7)]

    def far_start(p, near, copies, total, far):
        land(copies)
        acc = p[r, yl].astype(F32)
        for s in range(7):
            acc = acc + near[s].astype(F32)
        total[...] = acc.astype(BF16)
        return [trade(total, far.at[off - 1], at_z(4 * off, yl), far.at[off - 1]) for off in (2, 1, 3)]

    def far_sum(copies, total, far):
        land(copies)
        return total[...].astype(F32) + far[0].astype(F32) + far[1].astype(F32) + far[2].astype(F32)

    def spread_start(buf, h):
        base = slots(6)
        own = buf.at[r, yl]
        copies = []
        for i, step in enumerate((2, 1, -1)):
            for o in range(2):
                d = step if i else (-2 if o == h else 2)
                y = yl if o == 0 else 1 - yl
                s = base + 2 * i + o
                send(own, own, at_z(d, y), s, s)
                copies.append(coming(buf.at[(r - d + 4) % 4, y], s))
        return copies + [trade(own, own, y_mate, buf.at[r, 1 - yl])]

    def scatter_start(p, recv):
        return [
            trade(p.at[index_q(*o)], recv.at[i], (*index_q(*o), lat), recv.at[i]) for i, o in enumerate(others)
        ]

    def scatter_sum(copies, p, recv):
        acc = p[mp, tok].astype(F32)
        for i in reversed(range(15)):
            land([copies[i]])
            acc = acc + recv[i].astype(F32)
        return acc

    def gather_start(buf):
        own = buf.at[mp, tok]
        return [trade(own, own, (*index_q(*o), lat), buf.at[index_q(o[0], -o[1], o[2])]) for o in others]

    def split(v):
        v = v.reshape(8, 24, 256)
        return v[:, :, :128].astype(BF16), v[:, :, 128:].astype(BF16)

    def join(buf):
        return jnp.concatenate([flat(buf[0], 128), flat(buf[1], 128)], axis=1)

    def chain(h):
        pieces = [
            jnp.concatenate([xall[i // 2, i % 2, h, y].astype(F32) for y in range(2)], axis=0) for i in range(8)
        ]
        block = jnp.concatenate(pieces, axis=0).astype(BF16)
        fetched(1)
        part[h, 0] = dot(block, gate_ref[...]).reshape(4, 2, 24, 576).astype(BF16)
        cores = [trade(part.at[h, 0, :, 1 - core], bcore.at[h, 0], core_mate, bcore.at[h, 0])]
        fetched(2)
        part[h, 1] = dot(block, up_ref[...]).reshape(4, 2, 24, 576).astype(BF16)
        cores += [trade(part.at[h, 1, :, 1 - core], bcore.at[h, 1], core_mate, bcore.at[h, 1])]
        yield "b_dot"
        land(cores)
        for g in range(2):
            bsum[h, :, g] = (part[h, g, :, core].astype(F32) + bcore[h, g].astype(F32)).astype(BF16)
        across = [trade(bsum.at[h, (xc + d) % 4], brecv.at[h, d - 1], at_x(d), brecv.at[h, d - 1]) for d in (2, 1, 3)]
        yield "b_core"
        land(across)
        both = bsum[h, xc].astype(F32)
        for d in range(3):
            both = both + brecv[h, d].astype(F32)
        hid[h, xc, core] = (gelu(both[0]) * both[1]).astype(BF16)
        own = hid.at[h, xc, core]
        across = {d: trade(own, own, at_x(d), hid.at[h, (xc + 4 - d) % 4, core]) for d in (2, 1, 3)}
        cores = [trade(own, own, core_mate, hid.at[h, xc, 1 - core])]
        yield "b_x"
        for d in (1, 3, 2):
            land([across[d]])
            j = (xc + 4 - d) % 4
            cores.append(trade(hid.at[h, j, core], hid.at[h, j, core], core_mate, hid.at[h, j, 1 - core]))
        land(cores)

        fetched(3)
        dpart[h] = dot(flat(hid[h], 576), down_ref[...]).reshape(4, 2, 24, 576).astype(BF16)
        copies = reduce_start(dpart.at[h], dnear.at[h], h)
        yield "d_dot"
        copies = far_start(dpart.at[h], dnear.at[h], copies, dsum.at[h], dfar.at[h])
        yield "d_near"
        acts[h, r, yl] = far_sum(copies, dsum.at[h], dfar.at[h]).astype(BF16)
        copies = spread_start(acts.at[h], h)
        yield "d_far"
        land(copies)

        fetched(4, 5)
        fpart[h, 0], fpart[h, 1] = split(dot(flat(acts[h], 576), enc_ref[...]))
        copies = scatter_start(fpart.at[h], frecv.at[h])
        yield "e_near"
        bias = jnp.where(mp == 0, ebias_ref[:, :128], ebias_ref[:, 128:])
        pre = scatter_sum(copies, fpart.at[h], frecv.at[h]) + bias
        codes[h, mp, tok] = jnp.maximum(pre, 0.0).astype(BF16)
        copies = gather_start(codes.at[h])
        yield "f_rs"
        land(copies)

        fetched(6, 7)
        gpart[h] = dot(join(codes[h]), dect_ref[...], 1, 1).reshape(4, 2, 24, 576).astype(BF16)
        copies = reduce_start(gpart.at[h], gnear.at[h], h)
        yield "f_ag"
        copies = far_start(gpart.at[h], gnear.at[h], copies, gsum.at[h], gfar.at[h])
        yield "g_near"
        error = far_sum(copies, gsum.at[h], gfar.at[h]) + dbias_ref[...] - acts[h, r, yl].astype(F32)
        err[h, r, yl] = error.astype(BF16)
        copies = spread_start(err.at[h], h)
        yield "g_far"
        land(copies)

        ipart[h, 0], ipart[h, 1] = split(dot(flat(err[h], 576), dect_ref[...]))
        copies = scatter_start(ipart.at[h], irecv.at[h])
        yield "h_near"
        lgrad[h, mp, tok] = scatter_sum(copies, ipart.at[h], irecv.at[h]).astype(BF16)
        copies = gather_start(lgrad.at[h])
        yield "i_rs"
        if h == 0:
            gradt_ref[...] = dot(flat(err[0], 576), join(codes[0]), 0, 0)
        else:
            gradt_ref[...] += dot(flat(err[1], 576), join(codes[1]), 0, 0)
            rows = err[k % 2, r, k // 2].astype(F32)
            err_ref[...] = jnp.where(yl == 0, rows[0:12], rows[12:24]).reshape(12, 1, 576)
        yield "grad"
        land(copies)
        for c in range(2):
            for j in range(8):
                first = 24 * (4 * (2 * (j % 2) + h) + j // 2)
                lat_ref[first : first + 24, 128 * c : 128 * c + 128] = lgrad[h, c, j].astype(F32)

    fetched(0)
    pl.semaphore_wait(barrier, len(peers))

    gather_inputs(xall)
    for at in itertools.zip_longest(chain(0), chain(1)):
        pass
    finish()


def store(err_ref, gradt_ref, lat_ref, err_hbm, gradt_hbm, lat_hbm, sems):
    pairs = ((gradt_ref, gradt_hbm), (lat_ref, lat_hbm), (err_ref, err_hbm))
    copies = [pltpu.make_async_copy(src, dst, sems.at[i]) for i, (src, dst) in enumerate(pairs)]
    for copy in copies:
        copy.start()
    for copy in copies:
        copy.wait()


def body(inputs, gate_w, up_w, down_w, enc_w, enc_bias, dec_w, dec_bias):
    vmem = pl.BlockSpec(memory_space=pltpu.VMEM)
    reduce_scratch = [
        pltpu.VMEM((2, 4, 2, 24, 576), BF16), pltpu.VMEM((2, 7, 24, 576), BF16), pltpu.VMEM((2, 24, 576), BF16),
        pltpu.VMEM((2, 3, 24, 576), BF16), pltpu.VMEM((2, 4, 2, 24, 576), BF16),
    ]
    q_scratch = [
        pltpu.VMEM((2, 2, 8, 24, 128), BF16), pltpu.VMEM((2, 15, 24, 128), BF16), pltpu.VMEM((2, 2, 8, 24, 128), BF16)
    ]
    operands = (inputs[0], gate_w[0], up_w[0], down_w[0], enc_w[0], enc_bias[None], dec_w[:, 0, :].T, dec_bias)
    err, gradt, lat = pl.pallas_call(
        kernel,
        out_shape=(
            jax.ShapeDtypeStruct((12, 1, 576), F32),
            jax.ShapeDtypeStruct((576, 256), F32),
            jax.ShapeDtypeStruct((384, 256), F32),
        ),
        in_specs=[pl.BlockSpec(memory_space=pl.ANY)] * 8,
        out_specs=(vmem, vmem, vmem),
        scratch_shapes=[
            pltpu.VMEM((576, 576), BF16), pltpu.VMEM((576, 576), BF16), pltpu.VMEM((576, 576), BF16),
            pltpu.VMEM((576, 256), BF16), pltpu.VMEM((1, 256), F32),
            pltpu.VMEM((576, 256), BF16), pltpu.VMEM((1, 576), F32),
            pltpu.VMEM((4, 2, 2, 2, 12, 576), BF16),
            pltpu.VMEM((2, 2, 4, 2, 24, 576), BF16), pltpu.VMEM((2, 2, 4, 24, 576), BF16), pltpu.VMEM((2, 4, 2, 24, 576), BF16),
            pltpu.VMEM((2, 3, 2, 24, 576), BF16), pltpu.VMEM((2, 4, 2, 24, 576), BF16),
            *reduce_scratch, *reduce_scratch, *q_scratch, *q_scratch,
            pltpu.SemaphoreType.DMA((240,)), pltpu.SemaphoreType.DMA((240,)), pltpu.SemaphoreType.DMA((8,)),
        ],
        compiler_params=pltpu.CompilerParams(collective_id=0, has_side_effects=True, vmem_limit_bytes=40 << 20),
        name="step",
    )(
        *(pltpu.with_memory_space_constraint(v, pltpu.HBM) for v in operands)
    )
    hbm = pl.BlockSpec(memory_space=pl.ANY)
    err, gradt, lat = pl.pallas_call(
        store,
        out_shape=(
            jax.ShapeDtypeStruct((12, 1, 576), F32),
            jax.ShapeDtypeStruct((576, 256), F32),
            jax.ShapeDtypeStruct((384, 256), F32),
        ),
        in_specs=[hbm] * 3,
        out_specs=(hbm, hbm, hbm),
        scratch_shapes=[pltpu.SemaphoreType.DMA((3,))],
        compiler_params=pltpu.CompilerParams(vmem_limit_bytes=4 << 20),
        name="store",
    )(err, gradt, lat)
    return jnp.transpose(err, (1, 0, 2)), gradt.T[:, None, :], lat


def solution(mesh):
    in_specs = (
        P("mp", "lat", "tok"),
        P("mp", "tok", "lat"),
        P("mp", "tok", "lat"),
        P("mp", "lat", "tok"),
        P("mp", "tok", "lat"),
        P("lat"),
        P("lat", "mp", "tok"),
        P("mp", "tok"),
    )
    out_specs = (P("mp", "lat", "tok"), P("lat", "mp", "tok"), P(None, "lat"))
    return jax.shard_map(body, mesh=mesh, in_specs=in_specs, out_specs=out_specs, check_vma=False)
```
